32 devices in a mesh: grp: 8 (over y, x, core), top: 4 (over z).
Axes of the slice: x: 2, y: 2, z: 4, core: 2. Of those that a mesh axis runs over, the one named last changes fastest.
Arguments:
- basis_grad: float32 [8, 4, 512, 384], P('grp', 'top'), may hold values from -6 to 6
- leaf_q: float32 [8, 4, 512, 384], P('grp', 'top'), may hold values from -0.25 to 0.25
- leaf_rinv: float32 [8, 4, 384, 384], P('grp', 'top'), may hold values from -5 to 4, as said below
- merge_q1: float32 [8, 4, 384, 384], P('grp', 'top'), may hold values from -0.3125 to 0.3125
- merge_q2: float32 [4, 384, 384], P('top', 'grp'), may hold values from -0.15625 to 0.15625
Outputs:
- data_grad: float32 [8, 4, 512, 384], P('grp', 'top')
The draws below stay inside these ranges and needn't reach their ends.
Inputs may be any that keep to these rules, and one draw needn't show every extreme that they name: Each leaf_rinv[i,g] is upper triangular with a diagonal between 1 and 4.
All inputs are finite; a program needn't handle non-finite values.
Results may differ from the reference program's by a relative error of at most 0.00023.
Values sent between devices are 32-bit elements; how exact they have to be, the bound alone decides.
A program may use at most 64 MiB of HBM per device.

```python
import math
import jax
import jax.numpy as jnp
from jax import lax

W = 384
LEAF_ROWS = 512
GROUP_LEAVES = 8
GROUPS = 4


def draw_leaf_rinv(key, part):
    first_key, second_key = jax.random.split(key)
    shape = (GROUP_LEAVES, GROUPS, W, W)
    row_index = lax.broadcasted_iota(jnp.int32, shape, 2)
    col_index = lax.broadcasted_iota(jnp.int32, shape, 3)
    upper = jnp.clip(jax.random.normal(first_key, shape, jnp.float32), -5.0, 5.0) / math.sqrt(W)
    diagonal = jnp.exp(jax.random.uniform(second_key, shape, jnp.float32, 0.0, math.log(4.0)))
    zeros = jnp.zeros(shape, jnp.float32)
    return jnp.where(col_index > row_index, upper, jnp.where(col_index == row_index, diagonal, zeros))


def shard_levels(stream_key, dims, shards, low, largest):
    def one(axis_at, parts):
        heights = jax.random.uniform(jax.random.fold_in(jax.random.fold_in(stream_key, 6), axis_at), (parts,), jnp.float32, low / len(shards), largest / len(shards))
        return jnp.repeat(jnp.exp(heights), dims[axis_at] // parts).reshape((-1,) + (1,) * (len(dims) - axis_at - 1))

    level = one(*shards[0])
    for cut in shards[1:]:
        level = level * one(*cut)
    return level


def bell_draw(key, extent, spread, limit, cuts=(), dtype=jnp.bfloat16):
    array = spread * jax.random.normal(key, extent, jnp.float32)
    if cuts:
        array = array * shard_levels(key, extent, cuts, -0.22, 0.18)
    return jnp.clip(array, -limit, limit).astype(dtype)


def setup_inputs(seed: int = 0) -> dict:
    key_of = jax.random.split(jax.random.key(seed), 6)
    basis_grad = bell_draw(key_of[0], (GROUP_LEAVES, GROUPS, LEAF_ROWS, W), 1.0, 6.0, ((0, 8), (1, 4)), jnp.float32)
    leaf_q = bell_draw(key_of[1], (GROUP_LEAVES, GROUPS, LEAF_ROWS, W), LEAF_ROWS ** -0.5, 0.25, ((0, 8), (1, 4)), jnp.float32)
    leaf_rinv = draw_leaf_rinv(jax.random.fold_in(key_of[5], 71), 0)
    merge_q1 = bell_draw(key_of[3], (GROUP_LEAVES, GROUPS, W, W), W ** -0.5, 0.3125, ((0, 8), (1, 4)), jnp.float32)
    merge_q2 = bell_draw(key_of[4], (GROUPS, W, W), (W * GROUPS) ** -0.5, 0.15625, ((0, 4), (1, 8)), jnp.float32)
    return dict(basis_grad=basis_grad, leaf_q=leaf_q, leaf_rinv=leaf_rinv, merge_q1=merge_q1, merge_q2=merge_q2)


highest = lax.Precision.HIGHEST


def symmetrize(matrix):
    return jnp.tril(matrix) + jnp.swapaxes(jnp.tril(matrix, -1), -1, -2)


def contract(formula, former, latter):
    return jnp.einsum(formula, former.astype(jnp.float32), latter.astype(jnp.float32), precision=highest)


def reference(basis_grad, leaf_q, leaf_rinv, merge_q1, merge_q2):
    projected = contract("igra,igrb->igab", leaf_q, basis_grad)
    combined = contract("igab,gbc->igac", merge_q1, merge_q2)
    leaf_cotan = contract("igrc,igac->igra", basis_grad, combined)
    first_cotan = contract("igac,gbc->igab", projected, merge_q2)
    second_cotan = contract("igba,igbc->gac", merge_q1, projected)
    top_adjoint = -contract("gba,gbc->ac", second_cotan, merge_q2)
    top_sym = symmetrize(top_adjoint)
    group_back = contract("gab,gcb->gac", second_cotan + contract("gab,bc->gac", merge_q2, top_sym), merge_q2)
    group_adjoint = jnp.swapaxes(group_back, -1, -2) - contract("igba,igbc->gac", first_cotan, merge_q1)
    group_sym = symmetrize(group_adjoint)
    leaf_back = contract("igab,igcb->igac", first_cotan + contract("igab,gbc->igac", merge_q1, group_sym), merge_q1)
    leaf_adjoint = jnp.swapaxes(leaf_back, -1, -2) - contract("igra,igrc->igac", leaf_cotan, leaf_q)
    leaf_sym = symmetrize(leaf_adjoint)
    inner = leaf_cotan + contract("igra,igac->igrc", leaf_q, leaf_sym)
    return contract("igra,igca->igrc", inner, leaf_rinv)
```

```python
import jax
import jax.numpy as jnp
from jax import lax
from jax.sharding import PartitionSpec as P


def product(former, latter, former_dim, latter_dim):
    return lax.dot_general(
        former,
        latter,
        (((former_dim,), (latter_dim,)), ((), ())),
        precision=lax.Precision.HIGH,
        preferred_element_type=jnp.float32,
    )


def symmetrize(matrix):
    return jnp.tril(matrix) + jnp.tril(matrix, -1).T


def per_device(basis_grad, leaf_q, leaf_rinv, merge_q1, merge_q2):
    cotangent = basis_grad[0, 0]
    leaf_basis = leaf_q[0, 0]
    inverse = leaf_rinv[0, 0]
    first_block = merge_q1[0, 0]
    second_factor = lax.all_gather(merge_q2[0], "grp", axis=0, tiled=True)
    projected = product(leaf_basis, cotangent, 0, 0)
    combined = product(first_block, second_factor, 1, 0)
    top_adjoint = -lax.psum(product(projected, combined, 0, 0), ("grp", "top"))
    top_sym = symmetrize(top_adjoint)
    spread = product(leaf_basis, combined, 1, 0)
    outer = product(inverse, combined, 1, 0)
    inner = cotangent + product(spread, top_sym, 1, 0)
    result = product(inner, outer, 1, 1)
    return result[None, None]


def solution(mesh):
    placed = (
        P("grp", "top", None, None),
        P("grp", "top", None, None),
        P("grp", "top", None, None),
        P("grp", "top", None, None),
        P("top", "grp", None),
    )
    return jax.shard_map(
        per_device,
        mesh=mesh,
        in_specs=placed,
        out_specs=P("grp", "top", None, None),
        check_vma=False,
    )
```

```python
import functools

import jax
import jax.numpy as jnp
from jax import lax
from jax.experimental import pallas as pl
from jax.experimental.pallas import tpu as pltpu
from jax.sharding import PartitionSpec as P

MESH = pl.DeviceIdType.MESH
TILE = 128
f32 = jnp.float32
bf16 = jnp.bfloat16


def split(value, high, low):
    top = value.astype(bf16)
    high[...] = top
    low[...] = (value - top.astype(f32)).astype(bf16)


def dot(former, latter, latter_dim):
    return lax.dot_general(
        former, latter, (((1,), (latter_dim,)), ((), ())), preferred_element_type=f32
    )


def product(former, latter, latter_dim=0):
    former_high, former_low = former
    latter_high, latter_low = latter
    total = dot(former_high[...], latter_low[...], latter_dim)
    total += dot(former_low[...], latter_high[...], latter_dim)
    return total + dot(former_high[...], latter_high[...], latter_dim)


def kernel(
    n, m,
    b_hbm, q_hbm, r_hbm, m1_hbm, m2_hbm, o_ref,
    b, q, r, m1, m2_parts, m2,
    bh, bl, bth, btl, qh, ql, rh, rl, m1h, m1l, m2h, m2l,
    wh, wl, ch, cl, dh, dl, th, tl, yh, yl,
    packed, scatter, slab_sum, across, total,
    load_sem, m2_send, m2_recv, rs_send, rs_recv, z_send, z_recv, ag_send, ag_recv,
):
    me = lax.axis_index("grp")
    my_top = lax.axis_index("top")
    width = m1.shape[0]
    blocks = width // TILE
    part = m2_parts.shape[1]
    slab = slab_sum.shape[0]

    loads = [
        pltpu.make_async_copy(src, dst, load_sem.at[at])
        for at, (src, dst) in enumerate(
            (
                (b_hbm.at[0, 0], b),
                (q_hbm.at[0, 0], q),
                (m1_hbm.at[0, 0], m1),
                (r_hbm.at[0, 0], r),
                (m2_hbm.at[0], m2_parts.at[me]),
            )
        )
    ]
    for load in loads:
        load.start()

    barrier = pltpu.get_barrier_semaphore()
    for k in range(1, n):
        pl.semaphore_signal(
            barrier, inc=1, device_id={"grp": lax.rem(me + k, n)}, device_id_type=MESH
        )
    for k in range(1, m):
        pl.semaphore_signal(
            barrier, inc=1, device_id={"top": lax.rem(my_top + k, m)}, device_id_type=MESH
        )
    pl.semaphore_wait(barrier, n + m - 2)

    def spread(axis, at, size, source, target, send, recv):
        copies = []
        for k in range(1, size):
            peer = lax.rem(at + k, size)
            copy = pltpu.make_async_remote_copy(
                src_ref=source(peer),
                dst_ref=target(k),
                send_sem=send.at[k - 1],
                recv_sem=recv.at[k - 1],
                device_id={axis: peer},
                device_id_type=MESH,
            )
            copy.start()
            copies.append(copy)
        return copies

    gather = spread(
        "grp", me, n, lambda peer: m2_hbm.at[0], lambda k: m2_parts.at[me], m2_send, m2_recv
    )

    loads[0].wait()
    split(b[...].T, bth, btl)
    loads[1].wait()
    split(q[...], qh, ql)
    split(product((bth, btl), (qh, ql)), wh, wl)
    loads[2].wait()
    split(m1[...], m1h, m1l)
    split(product((wh, wl), (m1h, m1l)), wh, wl)

    loads[4].wait()
    for copy in gather:
        copy.wait_recv()
    for j in range(n):
        m2[j * part:(j + 1) * part, :] = m2_parts[j]
    split(m2[...], m2h, m2l)
    for i in range(blocks):
        rows = pl.ds(i * TILE, TILE)
        columns = pl.ds(0, (i + 1) * TILE)
        row = product(
            (wh.at[rows, :], wl.at[rows, :]), (m2h.at[:, columns], m2l.at[:, columns])
        )
        for j in range(i + 1):
            packed[pl.ds((i * (i + 1) // 2 + j) * TILE, TILE), :] = row[:, j * TILE:(j + 1) * TILE]

    def part_of(ref, at):
        return ref.at[pl.ds(pl.multiple_of(at * slab, 8), slab), :]

    reduce = spread(
        "grp", me, n, lambda peer: part_of(packed, peer), lambda k: scatter.at[k - 1], rs_send, rs_recv
    )
    split(product((m1h, m1l), (m2h, m2l)), ch, cl)
    value = packed[pl.ds(pl.multiple_of(me * slab, 8), slab), :]
    for k, copy in enumerate(reduce):
        copy.wait_recv()
        value += scatter[k]
    slab_sum[...] = value
    over = spread(
        "top", my_top, m, lambda peer: slab_sum, lambda k: across.at[k - 1], z_send, z_recv
    )
    split(product((qh, ql), (ch, cl)), yh, yl)
    for k, copy in enumerate(over):
        copy.wait_recv()
        value += across[k]
    total[pl.ds(pl.multiple_of(me * slab, 8), slab), :] = value
    share = spread(
        "grp", me, n, lambda peer: part_of(total, me), lambda k: part_of(total, me), ag_send, ag_recv
    )
    loads[3].wait()
    split(r[...], rh, rl)
    split(product((rh, rl), (ch, cl)), dh, dl)
    split(b[...], bh, bl)
    o_ref[...] = product((bh, bl), (dh, dl), 1)
    for copy in share:
        copy.wait_recv()

    row_at = lax.broadcasted_iota(jnp.int32, (TILE, TILE), 0)
    column_at = lax.broadcasted_iota(jnp.int32, (TILE, TILE), 1)
    for i in range(blocks):
        for j in range(i + 1):
            block = -total[pl.ds((i * (i + 1) // 2 + j) * TILE, TILE), :]
            if i == j:
                block = jnp.where(row_at >= column_at, block, block.T)
            here = (pl.ds(i * TILE, TILE), pl.ds(j * TILE, TILE))
            split(block, th.at[here], tl.at[here])
            if i != j:
                there = (pl.ds(j * TILE, TILE), pl.ds(i * TILE, TILE))
                split(block.T, th.at[there], tl.at[there])
    split(product((dh, dl), (th, tl)), wh, wl)
    o_ref[...] += product((yh, yl), (wh, wl), 1)

    for copies in (gather, reduce, over, share):
        for copy in copies:
            copy.wait_send()


def per_device(n, m, basis_grad, leaf_q, leaf_rinv, merge_q1, merge_q2):
    rows, width = basis_grad.shape[2:]
    part = merge_q2.shape[1]
    blocks = width // TILE
    length = blocks * (blocks + 1) // 2 * TILE
    slab = length // n
    square, tall = (width, width), (rows, width)

    def pair(shape):
        return [pltpu.VMEM(shape, bf16)] * 2

    def semaphores(count):
        return pltpu.SemaphoreType.DMA((max(count, 1),))

    result = pl.pallas_call(
        functools.partial(kernel, n, m),
        out_shape=jax.ShapeDtypeStruct(tall, f32),
        in_specs=[pl.BlockSpec(memory_space=pl.ANY)] * 5,
        out_specs=pl.BlockSpec(memory_space=pltpu.VMEM),
        scratch_shapes=[
            pltpu.VMEM(tall, f32),
            pltpu.VMEM(tall, f32),
            pltpu.VMEM(square, f32),
            pltpu.VMEM(square, f32),
            pltpu.VMEM((n, part, width), f32),
            pltpu.VMEM(square, f32),
            *pair(tall), *pair((width, rows)), *pair(tall), *pair(square), *pair(square), *pair(square),
            *pair(square), *pair(square), *pair(square), *pair(square), *pair(tall),
            pltpu.VMEM((length, TILE), f32),
            pltpu.VMEM((n - 1, slab, TILE), f32),
            pltpu.VMEM((slab, TILE), f32),
            pltpu.VMEM((m - 1, slab, TILE), f32),
            pltpu.VMEM((length, TILE), f32),
            semaphores(5),
            *[semaphores(n - 1)] * 4,
            *[semaphores(m - 1)] * 2,
            *[semaphores(n - 1)] * 2,
        ],
        compiler_params=pltpu.CompilerParams(
            collective_id=0, has_side_effects=True, vmem_limit_bytes=48 * 1024 * 1024
        ),
    )(basis_grad, leaf_q, leaf_rinv, merge_q1, merge_q2)
    return result[None, None]


def solution(mesh):
    placed = (
        P("grp", "top", None, None),
        P("grp", "top", None, None),
        P("grp", "top", None, None),
        P("grp", "top", None, None),
        P("top", "grp", None),
    )
    return jax.shard_map(
        functools.partial(per_device, mesh.shape["grp"], mesh.shape["top"]),
        mesh=mesh,
        in_specs=placed,
        out_specs=P("grp", "top", None, None),
        check_vma=False,
    )
```

```python
import functools

import jax
import jax.numpy as jnp
from jax import lax
from jax.experimental import pallas as pl
from jax.experimental.pallas import tpu as pltpu
from jax.sharding import PartitionSpec as P

MESH = pl.DeviceIdType.MESH
TILE = 128
VMEM_BYTES = 62 * 1024 * 1024
f32 = jnp.float32
bf16 = jnp.bfloat16


def split(value, high, low):
    top = value.astype(bf16)
    high[...] = top
    low[...] = (value - top.astype(f32)).astype(bf16)


def dot(former, latter, latter_dim):
    return lax.dot_general(
        former, latter, (((1,), (latter_dim,)), ((), ())), preferred_element_type=f32
    )


def product(former, latter, latter_dim=0):
    former_high, former_low = former
    latter_high, latter_low = latter
    total = dot(former_high[...], latter_low[...], latter_dim)
    total += dot(former_low[...], latter_high[...], latter_dim)
    return total + dot(former_high[...], latter_high[...], latter_dim)


def kernel(
    n, m,
    b_hbm, q_hbm, r_hbm, m1_hbm, m2_hbm, o_ref,
    b, q, r, m1, m2_parts, m2,
    bh, bl, bth, btl, qh, ql, rh, rl, m1h, m1l, m2h, m2l,
    wh, wl, ch, cl, dh, dl, th, tl, yh, yl,
    packed, folded, grp_in, top_in, grp_sum, top_sum, total,
    load_sem, own_send, own_recv, m2_send, m2_recv, pass_send, pass_recv, fold_send, fold_recv,
    grp_send, grp_recv, top_send, top_recv, share_send, share_recv, last_send, last_recv,
):
    me = lax.axis_index("grp")
    my_top = lax.axis_index("top")
    core = lax.rem(me, 2)
    chip = me // 2
    sibling = me + 1 - 2 * core
    width = m1.shape[0]
    blocks = width // TILE
    part = m2_parts.shape[1]
    half = packed.shape[0] // 2
    grp_slab = grp_sum.shape[0]
    top_slab = top_sum.shape[0]

    loads = [
        pltpu.make_async_copy(src, dst, load_sem.at[at])
        for at, (src, dst) in enumerate(
            (
                (b_hbm.at[0, 0], b),
                (q_hbm.at[0, 0], q),
                (m1_hbm.at[0, 0], m1),
                (r_hbm.at[0, 0], r),
                (m2_hbm.at[0], m2_parts.at[me]),
            )
        )
    ]
    for load in loads:
        load.start()

    def chip_peer(k):
        return {"grp": 2 * lax.rem(chip + k, n // 2) + core}

    def top_peer(k):
        return {"top": lax.rem(my_top + k, m)}

    other = {"grp": sibling}
    barrier = pltpu.get_barrier_semaphore()
    pl.semaphore_signal(barrier, inc=1, device_id=other, device_id_type=MESH)
    for k in range(1, n // 2):
        pl.semaphore_signal(barrier, inc=1, device_id=chip_peer(k), device_id_type=MESH)
    for k in range(1, m):
        pl.semaphore_signal(barrier, inc=1, device_id=top_peer(k), device_id_type=MESH)
    pl.semaphore_wait(barrier, n // 2 + m - 1)

    def remote(source, target, send, recv, peer):
        return pltpu.make_async_remote_copy(
            src_ref=source,
            dst_ref=target,
            send_sem=send,
            recv_sem=recv,
            device_id=peer,
            device_id_type=MESH,
        )

    def chips(source, target, send, recv):
        return [
            remote(source(lax.rem(chip + k, n // 2)), target(k), send.at[k - 1], recv.at[k - 1], chip_peer(k))
            for k in range(1, n // 2)
        ]

    def tops(source, target, send, recv):
        return [
            remote(source(lax.rem(my_top + k, m)), target(k), send.at[k - 1], recv.at[k - 1], top_peer(k))
            for k in range(1, m)
        ]

    def start(copies):
        for copy in copies:
            copy.start()

    def finish(copies):
        for copy in copies:
            copy.wait_send()

    gather = chips(lambda peer: m2_hbm.at[0], lambda k: m2_parts.at[me], m2_send, m2_recv)
    start(gather)
    own = remote(m2_hbm.at[0], m2_parts.at[me], own_send.at[0], own_recv.at[0], other)
    own.start()

    loads[0].wait()
    split(b[...].T, bth, btl)
    loads[1].wait()
    split(q[...], qh, ql)
    split(product((bth, btl), (qh, ql)), wh, wl)
    loads[2].wait()
    split(m1[...], m1h, m1l)
    split(product((wh, wl), (m1h, m1l)), wh, wl)

    passed = []
    for k, copy in enumerate(gather):
        copy.wait_recv()
        came = 2 * lax.rem(chip + n // 2 - k - 1, n // 2) + core
        passed.append(
            remote(m2_parts.at[came], m2_parts.at[came], pass_send.at[k], pass_recv.at[k], other)
        )
        passed[-1].start()
    loads[3].wait()
    split(r[...], rh, rl)
    split(b[...], bh, bl)
    loads[4].wait()
    own.wait_recv()
    for copy in passed:
        copy.wait_recv()
    for j in range(n):
        m2[j * part:(j + 1) * part, :] = m2_parts[j]
    split(m2[...], m2h, m2l)
    for i in range(blocks):
        rows = pl.ds(i * TILE, TILE)
        columns = pl.ds(0, (i + 1) * TILE)
        row = product(
            (wh.at[rows, :], wl.at[rows, :]), (m2h.at[:, columns], m2l.at[:, columns])
        )
        for j in range(i + 1):
            packed[pl.ds((i * (i + 1) // 2 + j) * TILE, TILE), :] = row[:, j * TILE:(j + 1) * TILE]

    fold = remote(
        packed.at[pl.ds(pl.multiple_of((1 - core) * half, 8), half), :],
        folded,
        fold_send.at[0],
        fold_recv.at[0],
        other,
    )
    fold.start()
    mine = pl.ds(pl.multiple_of(core * half, 8), half)

    def cut(ref, base, at, size):
        return ref.at[pl.ds(pl.multiple_of(base + at * size, 8), size), :]

    even_one = chips(
        lambda peer: cut(packed, 0, peer, grp_slab), lambda k: grp_in.at[k - 1, pl.ds(0, grp_slab)], grp_send, grp_recv
    )
    even_two = tops(lambda peer: grp_sum, lambda k: top_in.at[k - 1, pl.ds(0, grp_slab)], top_send, top_recv)
    even_three = chips(
        lambda peer: cut(total, 0, chip, grp_slab), lambda k: cut(total, 0, chip, grp_slab), share_send, share_recv
    )
    odd_one = tops(
        lambda peer: cut(packed, half, peer, top_slab), lambda k: top_in.at[k - 1, pl.ds(0, top_slab)], top_send, top_recv
    )
    odd_two = chips(lambda peer: top_sum, lambda k: grp_in.at[k - 1, pl.ds(0, top_slab)], grp_send, grp_recv)
    odd_three = tops(
        lambda peer: cut(total, half, my_top, top_slab), lambda k: cut(total, half, my_top, top_slab), share_send, share_recv
    )

    fold.wait()
    packed[mine, :] += folded[...]

    @pl.when(core == 0)
    def _():
        start(even_one)

    @pl.when(core == 1)
    def _():
        start(odd_one)

    split(product((m1h, m1l), (m2h, m2l)), ch, cl)

    @pl.when(core == 0)
    def _():
        value = packed[pl.ds(pl.multiple_of(chip * grp_slab, 8), grp_slab), :]
        for k, copy in enumerate(even_one):
            copy.wait_recv()
            value += grp_in[k, :grp_slab]
        grp_sum[...] = value
        start(even_two)

    @pl.when(core == 1)
    def _():
        value = packed[pl.ds(pl.multiple_of(half + my_top * top_slab, 8), top_slab), :]
        for k, copy in enumerate(odd_one):
            copy.wait_recv()
            value += top_in[k, :top_slab]
        top_sum[...] = value
        start(odd_two)

    split(product((qh, ql), (ch, cl)), yh, yl)

    @pl.when(core == 0)
    def _():
        value = grp_sum[...]
        for k, copy in enumerate(even_two):
            copy.wait_recv()
            value += top_in[k, :grp_slab]
        total[pl.ds(pl.multiple_of(chip * grp_slab, 8), grp_slab), :] = value
        start(even_three)

    @pl.when(core == 1)
    def _():
        value = top_sum[...]
        for k, copy in enumerate(odd_two):
            copy.wait_recv()
            value += grp_in[k, :top_slab]
        total[pl.ds(pl.multiple_of(half + my_top * top_slab, 8), top_slab), :] = value
        start(odd_three)

    split(product((rh, rl), (ch, cl)), dh, dl)
    o_ref[...] = product((bh, bl), (dh, dl), 1)

    last = remote(total.at[mine, :], total.at[mine, :], last_send.at[0], last_recv.at[0], other)

    @pl.when(core == 0)
    def _():
        for copy in even_three:
            copy.wait_recv()

    @pl.when(core == 1)
    def _():
        for copy in odd_three:
            copy.wait_recv()

    last.start()
    last.wait_recv()

    row_at = lax.broadcasted_iota(jnp.int32, (TILE, TILE), 0)
    column_at = lax.broadcasted_iota(jnp.int32, (TILE, TILE), 1)
    for i in range(blocks):
        for j in range(i + 1):
            block = -total[pl.ds((i * (i + 1) // 2 + j) * TILE, TILE), :]
            if i == j:
                block = jnp.where(row_at >= column_at, block, block.T)
            here = (pl.ds(i * TILE, TILE), pl.ds(j * TILE, TILE))
            split(block, th.at[here], tl.at[here])
            if i != j:
                there = (pl.ds(j * TILE, TILE), pl.ds(i * TILE, TILE))
                split(block.T, th.at[there], tl.at[there])
    split(product((dh, dl), (th, tl)), wh, wl)
    o_ref[...] += product((yh, yl), (wh, wl), 1)

    own.wait_send()
    last.wait_send()
    finish(gather)
    finish(passed)

    @pl.when(core == 0)
    def _():
        finish(even_one)
        finish(even_two)
        finish(even_three)

    @pl.when(core == 1)
    def _():
        finish(odd_one)
        finish(odd_two)
        finish(odd_three)


def per_device(n, m, basis_grad, leaf_q, leaf_rinv, merge_q1, merge_q2):
    rows, width = basis_grad.shape[2:]
    part = merge_q2.shape[1]
    blocks = width // TILE
    length = blocks * (blocks + 1) // 2 * TILE
    half = length // 2
    grp_slab = half // (n // 2)
    top_slab = half // m
    deep = max(grp_slab, top_slab)
    square, tall = (width, width), (rows, width)

    def pair(shape):
        return [pltpu.VMEM(shape, bf16)] * 2

    def semaphores(count):
        return pltpu.SemaphoreType.DMA((max(count, 1),))

    result = pl.pallas_call(
        functools.partial(kernel, n, m),
        out_shape=jax.ShapeDtypeStruct(tall, f32),
        in_specs=[pl.BlockSpec(memory_space=pl.ANY)] * 5,
        out_specs=pl.BlockSpec(memory_space=pltpu.VMEM),
        scratch_shapes=[
            pltpu.VMEM(tall, f32),
            pltpu.VMEM(tall, f32),
            pltpu.VMEM(square, f32),
            pltpu.VMEM(square, f32),
            pltpu.VMEM((n, part, width), f32),
            pltpu.VMEM(square, f32),
            *pair(tall), *pair((width, rows)), *pair(tall), *pair(square), *pair(square), *pair(square),
            *pair(square), *pair(square), *pair(square), *pair(square), *pair(tall),
            pltpu.VMEM((length, TILE), f32),
            pltpu.VMEM((half, TILE), f32),
            pltpu.VMEM((n // 2 - 1, deep, TILE), f32),
            pltpu.VMEM((m - 1, deep, TILE), f32),
            pltpu.VMEM((grp_slab, TILE), f32),
            pltpu.VMEM((top_slab, TILE), f32),
            pltpu.VMEM((length, TILE), f32),
            semaphores(5),
            *[semaphores(1)] * 2,
            *[semaphores(n // 2 - 1)] * 4,
            *[semaphores(1)] * 2,
            *[semaphores(n // 2 - 1)] * 2,
            *[semaphores(m - 1)] * 2,
            *[semaphores(max(n // 2, m) - 1)] * 2,
            *[semaphores(1)] * 2,
        ],
        compiler_params=pltpu.CompilerParams(
            collective_id=0, has_side_effects=True, vmem_limit_bytes=VMEM_BYTES
        ),
    )(basis_grad, leaf_q, leaf_rinv, merge_q1, merge_q2)
    return result[None, None]


def solution(mesh):
    placed = (
        P("grp", "top", None, None),
        P("grp", "top", None, None),
        P("grp", "top", None, None),
        P("grp", "top", None, None),
        P("top", "grp", None),
    )
    return jax.shard_map(
        functools.partial(per_device, mesh.shape["grp"], mesh.shape["top"]),
        mesh=mesh,
        in_specs=placed,
        out_specs=P("grp", "top", None, None),
        check_vma=False,
    )
```

```python
import functools

import jax
import jax.numpy as jnp
from jax import lax
from jax.experimental import pallas as pl
from jax.experimental.pallas import tpu as pltpu
from jax.sharding import PartitionSpec as P

MESH = pl.DeviceIdType.MESH
TILE = 128
VMEM_BYTES = 48 * 1024 * 1024
f32 = jnp.float32
bf16 = jnp.bfloat16


def split(value, high, low):
    top = value.astype(bf16)
    high[...] = top
    low[...] = (value - top.astype(f32)).astype(bf16)


def dot(former, latter, latter_dim):
    return lax.dot_general(
        former, latter, (((1,), (latter_dim,)), ((), ())), preferred_element_type=f32
    )


def product(former, latter, latter_dim=0):
    former_high, former_low = former
    latter_high, latter_low = latter
    total = dot(former_high[...], latter_low[...], latter_dim)
    total += dot(former_low[...], latter_high[...], latter_dim)
    return total + dot(former_high[...], latter_high[...], latter_dim)


def kernel(
    n, m,
    b_hbm, q_hbm, r_hbm, m1_hbm, m2_hbm, o_ref,
    b, q, r, m1, m2_parts, m2,
    bh, bl, bth, btl, qh, ql, rh, rl, m1h, m1l, m2h, m2l,
    wh, wl, ch, cl, dh, dl, th, tl, yh, yl,
    packed, mixed, folded, grp_in, top_in, grp_sum, top_sum, total,
    load_sem, own_send, own_recv, m2_send, m2_recv, pass_send, pass_recv, fold_send, fold_recv,
    grp_send, grp_recv, top_send, top_recv, share_send, share_recv, last_send, last_recv,
):
    me = lax.axis_index("grp")
    my_top = lax.axis_index("top")
    core = lax.rem(me, 2)
    chip = me // 2
    sibling = me + 1 - 2 * core
    width = m1.shape[0]
    blocks = width // TILE
    part = m2_parts.shape[1]
    half = packed.shape[0] // 2
    grp_slab = grp_sum.shape[0]
    top_slab = top_sum.shape[0]

    loads = [
        pltpu.make_async_copy(src, dst, load_sem.at[at])
        for at, (src, dst) in enumerate(
            (
                (b_hbm.at[0, 0], b),
                (q_hbm.at[0, 0], q),
                (m1_hbm.at[0, 0], m1),
                (r_hbm.at[0, 0], r),
                (m2_hbm.at[0], m2_parts.at[me]),
            )
        )
    ]
    for load in loads:
        load.start()

    def chip_peer(k):
        return {"grp": 2 * lax.rem(chip + k, n // 2) + core}

    def top_peer(k):
        return {"top": lax.rem(my_top + k, m)}

    other = {"grp": sibling}
    barrier = pltpu.get_barrier_semaphore()
    pl.semaphore_signal(barrier, inc=1, device_id=other, device_id_type=MESH)
    for k in range(1, n // 2):
        pl.semaphore_signal(barrier, inc=1, device_id=chip_peer(k), device_id_type=MESH)
    for k in range(1, m):
        pl.semaphore_signal(barrier, inc=1, device_id=top_peer(k), device_id_type=MESH)
    pl.semaphore_wait(barrier, n // 2 + m - 1)

    def remote(source, target, send, recv, peer):
        return pltpu.make_async_remote_copy(
            src_ref=source,
            dst_ref=target,
            send_sem=send,
            recv_sem=recv,
            device_id=peer,
            device_id_type=MESH,
        )

    def chips(source, target, send, recv):
        return [
            remote(source(lax.rem(chip + k, n // 2)), target(k), send.at[k - 1], recv.at[k - 1], chip_peer(k))
            for k in range(1, n // 2)
        ]

    def tops(source, target, send, recv):
        return [
            remote(source(lax.rem(my_top + k, m)), target(k), send.at[k - 1], recv.at[k - 1], top_peer(k))
            for k in range(1, m)
        ]

    def start(copies):
        for copy in copies:
            copy.start()

    def finish(copies):
        for copy in copies:
            copy.wait_send()

    gather = chips(lambda peer: m2_hbm.at[0], lambda k: m2_parts.at[me], m2_send, m2_recv)
    start(gather)
    own = remote(m2_hbm.at[0], m2_parts.at[me], own_send.at[0], own_recv.at[0], other)
    own.start()

    loads[0].wait()
    split(b[...].T, bth, btl)
    loads[1].wait()
    split(q[...], qh, ql)
    split(product((bth, btl), (qh, ql)), wh, wl)
    loads[2].wait()
    split(m1[...], m1h, m1l)
    mixed[...] = product((wh, wl), (m1h, m1l))
    cells = [(i, j) for i in range(blocks) for j in range(i + 1)]
    sides = cells[:len(cells) // 2], cells[len(cells) // 2:]
    spans = [pl.ds(side[0][0] * TILE, (side[-1][0] - side[0][0] + 1) * TILE) for side in sides]
    folds = [
        remote(mixed.at[span], folded.at[span], fold_send.at[0], fold_recv.at[0], other)
        for span in reversed(spans)
    ]
    for at in range(2):
        @pl.when(core == at)
        def _():
            folds[at].start()


    passed = []
    for k, copy in enumerate(gather):
        copy.wait_recv()
        came = 2 * lax.rem(chip + n // 2 - k - 1, n // 2) + core
        passed.append(
            remote(m2_parts.at[came], m2_parts.at[came], pass_send.at[k], pass_recv.at[k], other)
        )
        passed[-1].start()
    loads[3].wait()
    split(r[...], rh, rl)
    split(b[...], bh, bl)
    loads[4].wait()
    own.wait_recv()
    for copy in passed:
        copy.wait_recv()
    for j in range(n):
        m2[j * part:(j + 1) * part, :] = m2_parts[j]
    split(m2[...], m2h, m2l)
    for at in range(2):
        @pl.when(core == at)
        def _():
            folds[at].wait_send()
            folds[1 - at].wait_recv()
            split(mixed[spans[at]] + folded[spans[at]], wh.at[spans[at]], wl.at[spans[at]])
            for i in sorted({cell[0] for cell in sides[at]}):
                line = [cell[1] for cell in sides[at] if cell[0] == i]
                rows = pl.ds(i * TILE, TILE)
                columns = pl.ds(line[0] * TILE, len(line) * TILE)
                row = product(
                    (wh.at[rows, :], wl.at[rows, :]), (m2h.at[:, columns], m2l.at[:, columns])
                )
                for j in line:
                    packed[pl.ds(cells.index((i, j)) * TILE, TILE), :] = row[
                        :, (j - line[0]) * TILE:(j - line[0] + 1) * TILE
                    ]

    def cut(ref, base, at, size):
        return ref.at[pl.ds(pl.multiple_of(base + at * size, 8), size), :]

    even_one = chips(
        lambda peer: cut(packed, 0, peer, grp_slab), lambda k: grp_in.at[k - 1, pl.ds(0, grp_slab)], grp_send, grp_recv
    )
    even_two = tops(lambda peer: grp_sum, lambda k: top_in.at[k - 1, pl.ds(0, grp_slab)], top_send, top_recv)
    even_three = chips(
        lambda peer: cut(total, 0, chip, grp_slab), lambda k: cut(total, 0, chip, grp_slab), share_send, share_recv
    )
    odd_one = tops(
        lambda peer: cut(packed, half, peer, top_slab), lambda k: top_in.at[k - 1, pl.ds(0, top_slab)], top_send, top_recv
    )
    odd_two = chips(lambda peer: top_sum, lambda k: grp_in.at[k - 1, pl.ds(0, top_slab)], grp_send, grp_recv)
    odd_three = tops(
        lambda peer: cut(total, half, my_top, top_slab), lambda k: cut(total, half, my_top, top_slab), share_send, share_recv
    )

    even_last = [
        remote(
            cut(total, 0, lax.rem(chip + n // 2 - k, n // 2), grp_slab),
            cut(total, 0, lax.rem(chip + n // 2 - k, n // 2), grp_slab),
            last_send.at[k], last_recv.at[k], other,
        )
        for k in range(n // 2)
    ]
    odd_last = [
        remote(
            cut(total, half, lax.rem(my_top + m - k, m), top_slab),
            cut(total, half, lax.rem(my_top + m - k, m), top_slab),
            last_send.at[k], last_recv.at[k], other,
        )
        for k in range(m)
    ]

    @pl.when(core == 0)
    def _():
        start(even_one)

    @pl.when(core == 1)
    def _():
        start(odd_one)

    split(product((m1h, m1l), (m2h, m2l)), ch, cl)

    @pl.when(core == 0)
    def _():
        value = packed[pl.ds(pl.multiple_of(chip * grp_slab, 8), grp_slab), :]
        for k, copy in enumerate(even_one):
            copy.wait_recv()
            value += grp_in[k, :grp_slab]
        grp_sum[...] = value
        start(even_two)

    @pl.when(core == 1)
    def _():
        value = packed[pl.ds(pl.multiple_of(half + my_top * top_slab, 8), top_slab), :]
        for k, copy in enumerate(odd_one):
            copy.wait_recv()
            value += top_in[k, :top_slab]
        top_sum[...] = value
        start(odd_two)

    split(product((qh, ql), (ch, cl)), yh, yl)

    @pl.when(core == 0)
    def _():
        value = grp_sum[...]
        for k, copy in enumerate(even_two):
            copy.wait_recv()
            value += top_in[k, :grp_slab]
        total[pl.ds(pl.multiple_of(chip * grp_slab, 8), grp_slab), :] = value
        start(even_three)
        even_last[0].start()

    @pl.when(core == 1)
    def _():
        value = top_sum[...]
        for k, copy in enumerate(odd_two):
            copy.wait_recv()
            value += grp_in[k, :top_slab]
        total[pl.ds(pl.multiple_of(half + my_top * top_slab, 8), top_slab), :] = value
        start(odd_three)
        odd_last[0].start()

    split(product((rh, rl), (ch, cl)), dh, dl)
    o_ref[...] = product((bh, bl), (dh, dl), 1)

    @pl.when(core == 0)
    def _():
        for k, copy in enumerate(even_three):
            copy.wait_recv()
            even_last[k + 1].start()
        for copy in odd_last:
            copy.wait_recv()

    @pl.when(core == 1)
    def _():
        for k, copy in enumerate(odd_three):
            copy.wait_recv()
            odd_last[k + 1].start()
        for copy in even_last:
            copy.wait_recv()

    row_at = lax.broadcasted_iota(jnp.int32, (TILE, TILE), 0)
    column_at = lax.broadcasted_iota(jnp.int32, (TILE, TILE), 1)
    for i in range(blocks):
        for j in range(i + 1):
            block = -total[pl.ds((i * (i + 1) // 2 + j) * TILE, TILE), :]
            if i == j:
                block = jnp.where(row_at >= column_at, block, block.T)
            here = (pl.ds(i * TILE, TILE), pl.ds(j * TILE, TILE))
            split(block, th.at[here], tl.at[here])
            if i != j:
                there = (pl.ds(j * TILE, TILE), pl.ds(i * TILE, TILE))
                split(block.T, th.at[there], tl.at[there])
    split(product((dh, dl), (th, tl)), wh, wl)
    o_ref[...] += product((yh, yl), (wh, wl), 1)

    own.wait_send()
    finish(gather)
    finish(passed)

    @pl.when(core == 0)
    def _():
        finish(even_one)
        finish(even_two)
        finish(even_three)
        finish(even_last)

    @pl.when(core == 1)
    def _():
        finish(odd_one)
        finish(odd_two)
        finish(odd_three)
        finish(odd_last)


def per_device(n, m, basis_grad, leaf_q, leaf_rinv, merge_q1, merge_q2):
    rows, width = basis_grad.shape[2:]
    part = merge_q2.shape[1]
    blocks = width // TILE
    length = blocks * (blocks + 1) // 2 * TILE
    half = length // 2
    grp_slab = half // (n // 2)
    top_slab = half // m
    deep = max(grp_slab, top_slab)
    square, tall = (width, width), (rows, width)

    def pair(shape):
        return [pltpu.VMEM(shape, bf16)] * 2

    def semaphores(count):
        return pltpu.SemaphoreType.DMA((max(count, 1),))

    basis_grad, leaf_q, leaf_rinv, merge_q1, merge_q2 = (
        pltpu.with_memory_space_constraint(value, pltpu.HBM)
        for value in (basis_grad, leaf_q, leaf_rinv, merge_q1, merge_q2)
    )
    result = pl.pallas_call(
        functools.partial(kernel, n, m),
        out_shape=jax.ShapeDtypeStruct(tall, f32),
        in_specs=[pl.BlockSpec(memory_space=pl.ANY)] * 5,
        out_specs=pl.BlockSpec(memory_space=pltpu.VMEM),
        scratch_shapes=[
            pltpu.VMEM(tall, f32),
            pltpu.VMEM(tall, f32),
            pltpu.VMEM(square, f32),
            pltpu.VMEM(square, f32),
            pltpu.VMEM((n, part, width), f32),
            pltpu.VMEM(square, f32),
            *pair(tall), *pair((width, rows)), *pair(tall), *pair(square), *pair(square), *pair(square),
            *pair(square), *pair(square), *pair(square), *pair(square), *pair(tall),
            pltpu.VMEM((length, TILE), f32),
            pltpu.VMEM(square, f32),
            pltpu.VMEM(square, f32),
            pltpu.VMEM((n // 2 - 1, deep, TILE), f32),
            pltpu.VMEM((m - 1, deep, TILE), f32),
            pltpu.VMEM((grp_slab, TILE), f32),
            pltpu.VMEM((top_slab, TILE), f32),
            pltpu.VMEM((length, TILE), f32),
            semaphores(5),
            *[semaphores(1)] * 2,
            *[semaphores(n // 2 - 1)] * 4,
            *[semaphores(1)] * 2,
            *[semaphores(n // 2 - 1)] * 2,
            *[semaphores(m - 1)] * 2,
            *[semaphores(max(n // 2, m) - 1)] * 2,
            *[semaphores(max(n // 2, m))] * 2,
        ],
        compiler_params=pltpu.CompilerParams(
            collective_id=0, has_side_effects=True, vmem_limit_bytes=VMEM_BYTES
        ),
    )(basis_grad, leaf_q, leaf_rinv, merge_q1, merge_q2)
    return result[None, None]


def solution(mesh):
    placed = (
        P("grp", "top", None, None),
        P("grp", "top", None, None),
        P("grp", "top", None, None),
        P("grp", "top", None, None),
        P("top", "grp", None),
    )
    return jax.shard_map(
        functools.partial(per_device, mesh.shape["grp"], mesh.shape["top"]),
        mesh=mesh,
        in_specs=placed,
        out_specs=P("grp", "top", None, None),
        check_vma=False,
    )
```

```python
import functools

import jax
import jax.numpy as jnp
from jax import lax
from jax.experimental import pallas as pl
from jax.experimental.pallas import tpu as pltpu
from jax.sharding import PartitionSpec as P

MESH = pl.DeviceIdType.MESH
TILE = 128
VMEM_BYTES = 48 * 1024 * 1024
f32 = jnp.float32
bf16 = jnp.bfloat16


def split(value, high, low):
    top = value.astype(bf16)
    high[...] = top
    low[...] = (value - top.astype(f32)).astype(bf16)


def dot(former, latter, latter_dim):
    return lax.dot_general(
        former, latter, (((1,), (latter_dim,)), ((), ())), preferred_element_type=f32
    )


def product(former, latter, latter_dim=0):
    former_high, former_low = former
    latter_high, latter_low = latter
    high, other = former_high[...], latter_high[...]
    left = jnp.concatenate([high, former_low[...], high], axis=1)
    right = jnp.concatenate([latter_low[...], other, other], axis=latter_dim)
    return dot(left, right, latter_dim)


def kernel(
    n, m,
    b_hbm, q_hbm, r_hbm, m1_hbm, m2_hbm, o_ref,
    b, q, r, m1, m2_parts, m2,
    bh, bl, bth, btl, qh, ql, rh, rl, m1h, m1l, m2h, m2l,
    wh, wl, ch, cl, dh, dl, th, tl, yh, yl,
    packed, mixed, folded, grp_in, top_in, grp_sum, top_sum, total,
    load_sem, own_send, own_recv, m2_send, m2_recv, pass_send, pass_recv, fold_send, fold_recv,
    grp_send, grp_recv, top_send, top_recv, share_send, share_recv, last_send, last_recv,
):
    me = lax.axis_index("grp")
    my_top = lax.axis_index("top")
    core = lax.rem(me, 2)
    chip = me // 2
    sibling = me + 1 - 2 * core
    width = m1.shape[0]
    blocks = width // TILE
    part = m2_parts.shape[1]
    half = packed.shape[0] // 2
    grp_slab = grp_sum.shape[0]
    top_slab = top_sum.shape[0]

    loads = [
        pltpu.make_async_copy(src, dst, load_sem.at[at])
        for at, (src, dst) in enumerate(
            (
                (b_hbm.at[0, 0], b),
                (q_hbm.at[0, 0], q),
                (m1_hbm.at[0, 0], m1),
                (r_hbm.at[0, 0], r),
                (m2_hbm.at[0], m2_parts.at[me]),
            )
        )
    ]
    for load in loads:
        load.start()

    def chip_peer(k):
        return {"grp": 2 * lax.rem(chip + k, n // 2) + core}

    def top_peer(k):
        return {"top": lax.rem(my_top + k, m)}

    other = {"grp": sibling}
    barrier = pltpu.get_barrier_semaphore()
    pl.semaphore_signal(barrier, inc=1, device_id=other, device_id_type=MESH)
    for k in range(1, n // 2):
        pl.semaphore_signal(barrier, inc=1, device_id=chip_peer(k), device_id_type=MESH)
    for k in range(1, m):
        pl.semaphore_signal(barrier, inc=1, device_id=top_peer(k), device_id_type=MESH)
    pl.semaphore_wait(barrier, n // 2 + m - 1)

    def remote(source, target, send, recv, peer):
        return pltpu.make_async_remote_copy(
            src_ref=source,
            dst_ref=target,
            send_sem=send,
            recv_sem=recv,
            device_id=peer,
            device_id_type=MESH,
        )

    def chips(source, target, send, recv):
        return [
            remote(source(lax.rem(chip + k, n // 2)), target(k), send.at[k - 1], recv.at[k - 1], chip_peer(k))
            for k in range(1, n // 2)
        ]

    def tops(source, target, send, recv):
        return [
            remote(source(lax.rem(my_top + k, m)), target(k), send.at[k - 1], recv.at[k - 1], top_peer(k))
            for k in range(1, m)
        ]

    def start(copies):
        for copy in copies:
            copy.start()

    def finish(copies):
        for copy in copies:
            copy.wait_send()

    gather = chips(lambda peer: m2_hbm.at[0], lambda k: m2_parts.at[me], m2_send, m2_recv)
    start(gather)
    own = remote(m2_hbm.at[0], m2_parts.at[me], own_send.at[0], own_recv.at[0], other)
    own.start()

    loads[0].wait()
    split(b[...].T, bth, btl)
    loads[1].wait()
    split(q[...], qh, ql)
    split(product((bth, btl), (qh, ql)), wh, wl)
    loads[2].wait()
    split(m1[...], m1h, m1l)
    mixed[...] = product((wh, wl), (m1h, m1l))
    cells = [(i, j) for i in range(blocks) for j in range(i + 1)]
    sides = cells[:len(cells) // 2], cells[len(cells) // 2:]
    spans = [pl.ds(side[0][0] * TILE, (side[-1][0] - side[0][0] + 1) * TILE) for side in sides]
    folds = [
        remote(mixed.at[span], folded.at[span], fold_send.at[0], fold_recv.at[0], other)
        for span in reversed(spans)
    ]
    for at in range(2):
        @pl.when(core == at)
        def _():
            folds[at].start()


    passed = []
    for k, copy in enumerate(gather):
        copy.wait_recv()
        came = 2 * lax.rem(chip + n // 2 - k - 1, n // 2) + core
        passed.append(
            remote(m2_parts.at[came], m2_parts.at[came], pass_send.at[k], pass_recv.at[k], other)
        )
        passed[-1].start()
    loads[3].wait()
    split(r[...], rh, rl)
    split(b[...], bh, bl)
    loads[4].wait()
    own.wait_recv()
    for copy in passed:
        copy.wait_recv()
    for j in range(n):
        m2[j * part:(j + 1) * part, :] = m2_parts[j]
    split(m2[...], m2h, m2l)
    for at in range(2):
        @pl.when(core == at)
        def _():
            folds[at].wait_send()
            folds[1 - at].wait_recv()
            split(mixed[spans[at]] + folded[spans[at]], wh.at[spans[at]], wl.at[spans[at]])
            for i in sorted({cell[0] for cell in sides[at]}):
                line = [cell[1] for cell in sides[at] if cell[0] == i]
                rows = pl.ds(i * TILE, TILE)
                columns = pl.ds(line[0] * TILE, len(line) * TILE)
                row = product(
                    (wh.at[rows, :], wl.at[rows, :]), (m2h.at[:, columns], m2l.at[:, columns])
                )
                for j in line:
                    packed[pl.ds(cells.index((i, j)) * TILE, TILE), :] = row[
                        :, (j - line[0]) * TILE:(j - line[0] + 1) * TILE
                    ]

    def cut(ref, base, at, size):
        return ref.at[pl.ds(pl.multiple_of(base + at * size, 8), size), :]

    even_one = chips(
        lambda peer: cut(packed, 0, peer, grp_slab), lambda k: grp_in.at[k - 1, pl.ds(0, grp_slab)], grp_send, grp_recv
    )
    even_two = tops(lambda peer: grp_sum, lambda k: top_in.at[k - 1, pl.ds(0, grp_slab)], top_send, top_recv)
    even_three = chips(
        lambda peer: cut(total, 0, chip, grp_slab), lambda k: cut(total, 0, chip, grp_slab), share_send, share_recv
    )
    odd_one = tops(
        lambda peer: cut(packed, half, peer, top_slab), lambda k: top_in.at[k - 1, pl.ds(0, top_slab)], top_send, top_recv
    )
    odd_two = chips(lambda peer: top_sum, lambda k: grp_in.at[k - 1, pl.ds(0, top_slab)], grp_send, grp_recv)
    odd_three = tops(
        lambda peer: cut(total, half, my_top, top_slab), lambda k: cut(total, half, my_top, top_slab), share_send, share_recv
    )

    even_last = [
        remote(
            cut(total, 0, lax.rem(chip + n // 2 - k, n // 2), grp_slab),
            cut(total, 0, lax.rem(chip + n // 2 - k, n // 2), grp_slab),
            last_send.at[k], last_recv.at[k], other,
        )
        for k in range(n // 2)
    ]
    odd_last = [
        remote(
            cut(total, half, lax.rem(my_top + m - k, m), top_slab),
            cut(total, half, lax.rem(my_top + m - k, m), top_slab),
            last_send.at[k], last_recv.at[k], other,
        )
        for k in range(m)
    ]

    @pl.when(core == 0)
    def _():
        start(even_one)

    @pl.when(core == 1)
    def _():
        start(odd_one)

    split(product((m1h, m1l), (m2h, m2l)), ch, cl)

    @pl.when(core == 0)
    def _():
        value = packed[pl.ds(pl.multiple_of(chip * grp_slab, 8), grp_slab), :]
        for k, copy in enumerate(even_one):
            copy.wait_recv()
            value += grp_in[k, :grp_slab]
        grp_sum[...] = value
        start(even_two)

    @pl.when(core == 1)
    def _():
        value = packed[pl.ds(pl.multiple_of(half + my_top * top_slab, 8), top_slab), :]
        for k, copy in enumerate(odd_one):
            copy.wait_recv()
            value += top_in[k, :top_slab]
        top_sum[...] = value
        start(odd_two)

    split(product((qh, ql), (ch, cl)), yh, yl)

    @pl.when(core == 0)
    def _():
        value = grp_sum[...]
        for k, copy in enumerate(even_two):
            copy.wait_recv()
            value += top_in[k, :grp_slab]
        total[pl.ds(pl.multiple_of(chip * grp_slab, 8), grp_slab), :] = value
        start(even_three)
        even_last[0].start()

    @pl.when(core == 1)
    def _():
        value = top_sum[...]
        for k, copy in enumerate(odd_two):
            copy.wait_recv()
            value += grp_in[k, :top_slab]
        total[pl.ds(pl.multiple_of(half + my_top * top_slab, 8), top_slab), :] = value
        start(odd_three)
        odd_last[0].start()

    split(product((rh, rl), (ch, cl)), dh, dl)
    o_ref[...] = product((bh, bl), (dh, dl), 1)

    row_at = lax.broadcasted_iota(jnp.int32, (TILE, TILE), 0)
    column_at = lax.broadcasted_iota(jnp.int32, (TILE, TILE), 1)

    def assemble(side):
        for i, j in side:
            block = -total[pl.ds(cells.index((i, j)) * TILE, TILE), :]
            if i == j:
                block = jnp.where(row_at >= column_at, block, block.T)
            here = (pl.ds(i * TILE, TILE), pl.ds(j * TILE, TILE))
            split(block, th.at[here], tl.at[here])
            if i != j:
                there = (pl.ds(j * TILE, TILE), pl.ds(i * TILE, TILE))
                split(block.T, th.at[there], tl.at[there])

    @pl.when(core == 0)
    def _():
        for k, copy in enumerate(even_three):
            copy.wait_recv()
            even_last[k + 1].start()
        assemble(sides[0])
        for copy in odd_last:
            copy.wait_recv()
        assemble(sides[1])

    @pl.when(core == 1)
    def _():
        for k, copy in enumerate(odd_three):
            copy.wait_recv()
            odd_last[k + 1].start()
        assemble(sides[1])
        for copy in even_last:
            copy.wait_recv()
        assemble(sides[0])

    split(product((dh, dl), (th, tl)), wh, wl)
    o_ref[...] += product((yh, yl), (wh, wl), 1)

    own.wait_send()
    finish(gather)
    finish(passed)

    @pl.when(core == 0)
    def _():
        finish(even_one)
        finish(even_two)
        finish(even_three)
        finish(even_last)

    @pl.when(core == 1)
    def _():
        finish(odd_one)
        finish(odd_two)
        finish(odd_three)
        finish(odd_last)


def per_device(n, m, basis_grad, leaf_q, leaf_rinv, merge_q1, merge_q2):
    rows, width = basis_grad.shape[2:]
    part = merge_q2.shape[1]
    blocks = width // TILE
    length = blocks * (blocks + 1) // 2 * TILE
    half = length // 2
    grp_slab = half // (n // 2)
    top_slab = half // m
    deep = max(grp_slab, top_slab)
    square, tall = (width, width), (rows, width)

    def pair(shape):
        return [pltpu.VMEM(shape, bf16)] * 2

    def semaphores(count):
        return pltpu.SemaphoreType.DMA((max(count, 1),))

    basis_grad, leaf_q, leaf_rinv, merge_q1, merge_q2 = (
        pltpu.with_memory_space_constraint(value, pltpu.HBM)
        for value in (basis_grad, leaf_q, leaf_rinv, merge_q1, merge_q2)
    )
    result = pl.pallas_call(
        functools.partial(kernel, n, m),
        out_shape=jax.ShapeDtypeStruct(tall, f32),
        in_specs=[pl.BlockSpec(memory_space=pl.ANY)] * 5,
        out_specs=pl.BlockSpec(memory_space=pltpu.VMEM),
        scratch_shapes=[
            pltpu.VMEM(tall, f32),
            pltpu.VMEM(tall, f32),
            pltpu.VMEM(square, f32),
            pltpu.VMEM(square, f32),
            pltpu.VMEM((n, part, width), f32),
            pltpu.VMEM(square, f32),
            *pair(tall), *pair((width, rows)), *pair(tall), *pair(square), *pair(square), *pair(square),
            *pair(square), *pair(square), *pair(square), *pair(square), *pair(tall),
            pltpu.VMEM((length, TILE), f32),
            pltpu.VMEM(square, f32),
            pltpu.VMEM(square, f32),
            pltpu.VMEM((n // 2 - 1, deep, TILE), f32),
            pltpu.VMEM((m - 1, deep, TILE), f32),
            pltpu.VMEM((grp_slab, TILE), f32),
            pltpu.VMEM((top_slab, TILE), f32),
            pltpu.VMEM((length, TILE), f32),
            semaphores(5),
            *[semaphores(1)] * 2,
            *[semaphores(n // 2 - 1)] * 4,
            *[semaphores(1)] * 2,
            *[semaphores(n // 2 - 1)] * 2,
            *[semaphores(m - 1)] * 2,
            *[semaphores(max(n // 2, m) - 1)] * 2,
            *[semaphores(max(n // 2, m))] * 2,
        ],
        compiler_params=pltpu.CompilerParams(
            collective_id=0, has_side_effects=True, vmem_limit_bytes=VMEM_BYTES
        ),
    )(basis_grad, leaf_q, leaf_rinv, merge_q1, merge_q2)
    return result[None, None]


def solution(mesh):
    placed = (
        P("grp", "top", None, None),
        P("grp", "top", None, None),
        P("grp", "top", None, None),
        P("grp", "top", None, None),
        P("top", "grp", None),
    )
    return jax.shard_map(
        functools.partial(per_device, mesh.shape["grp"], mesh.shape["top"]),
        mesh=mesh,
        in_specs=placed,
        out_specs=P("grp", "top", None, None),
        check_vma=False,
    )
```
